32 devices in a mesh: groups: 2 (over y), blk: 4 (over z), rep: 4 (over x, core).
Axes of the slice: x: 2, y: 2, z: 4, core: 2. Of those that a mesh axis runs over, the one named last changes fastest.
Arguments:
- orbitals: float32 [8, 262144], P(('groups', 'blk')), parts along dimension 0, may hold values from -6 to 6
- offsets: int32 [8], P('groups'), parts along dimension 0, may hold values from 0 to 3
Outputs:
- exchanged: float32 [8, 262144], P(('groups', 'blk'), 'rep'), parts along dimension 0
- margin: float32 [8, 4], P(('groups', 'blk')), parts along dimension 0
The draws below stay inside these ranges and needn't reach their ends.
There are 2 independent parts, one for each index of `groups`. The reference program is written for one: setup_inputs(seed, part) draws one part's arguments, and reference() takes and returns one part's arrays. A program takes and returns all parts, laid end to end along the dimension named above; each array names one. Nothing has to cross between parts.
All inputs are finite; a program needn't handle non-finite values.
Results may differ from the reference program's by a relative error of at most 0.0001.
Values sent between devices are 32-bit elements; how exact they have to be, the bound alone decides.
A program may use at most 64 MiB of HBM per device.

```python
import jax
import jax.numpy as jnp
from jax import lax

NG = 64
OB = 1
STEPS = 3
NORB = 4
CELLS = 262144
N_BLK = 4
N_REP = 4


def set_ends(drawn, stream_key, smallest, top_value):
    index_at = [jax.random.randint(jax.random.fold_in(stream_key, axis), (), 0, length) for axis, length in enumerate(drawn.shape)]
    widest = drawn.shape.index(max(drawn.shape))
    beside = index_at[:widest] + [(index_at[widest] + 1) % drawn.shape[widest]] + index_at[widest + 1:]
    return drawn.at[tuple(index_at)].set(smallest).at[tuple(beside)].set(top_value)


def level_of(own_key, shape, shards, low, high):
    loudness = 1.0
    for axis_at, parts in shards:
        heights = jax.random.uniform(jax.random.fold_in(jax.random.fold_in(own_key, 6), axis_at), (parts,), jnp.float32, low / len(shards), high / len(shards))
        loudness = loudness * jnp.repeat(jnp.exp(heights), shape[axis_at] // parts).reshape((-1,) + (1,) * (len(shape) - 1 - axis_at))
    return loudness


def centred(stream_key, shape, deviation, reach, split=(), held_as=jnp.bfloat16):
    array = jax.random.normal(stream_key, shape, jnp.float32) * deviation
    if len(split) > 0:
        array = level_of(stream_key, shape, split, -0.22, 0.18) * array
    return jnp.clip(array, min=-reach, max=reach).astype(held_as)


def setup_inputs(seed: int = 0, part: int = 0) -> dict:
    splits = jax.random.split(jax.random.key(seed), 3)
    part_keys = jax.random.split(jax.random.fold_in(splits[2], part), 3)
    orbitals = centred(part_keys[0], (NORB, CELLS), 1.0, 6.0, ((0, 4),), jnp.float32)
    offsets = set_ends(jax.random.randint(part_keys[1], (N_REP,), 0, N_BLK), jax.random.fold_in(part_keys[1], 1), 0, N_BLK - 1).astype(jnp.int32)
    return {"orbitals": orbitals, "offsets": offsets}


precise_mode = lax.Precision.HIGHEST
screen_scale = 0.05


def cas_table(grid_points):
    grid_index = jnp.arange(grid_points, dtype=jnp.int32)
    product = (grid_index[:, None] * grid_index[None, :]) % grid_points
    phase_angle = (2.0 * jnp.pi / grid_points) * product.astype(jnp.float32)
    return jnp.cos(phase_angle) + jnp.sin(phase_angle)


def screened_kernel(grid_points):
    grid_index = jnp.arange(grid_points, dtype=jnp.int32)
    folded = jnp.where(grid_index <= grid_points // 2, grid_index, grid_index - grid_points).astype(jnp.float32)
    squares = folded * folded
    k_squared = squares[:, None, None] + squares[None, :, None] + squares[None, None, :]
    safe_square = jnp.maximum(k_squared, 1.0)
    screened = (4.0 * jnp.pi / (screen_scale * safe_square)) * (1.0 - jnp.exp(-screen_scale * safe_square / (4.0 * jnp.pi)))
    return jnp.where(k_squared > 0.5, screened, jnp.ones_like(screened))


def hartley_cube(values_field, cas_values):
    values_field = jnp.einsum('kx,abxyz->abkyz', cas_values, values_field, precision=precise_mode)
    values_field = jnp.einsum('ky,abxyz->abxkz', cas_values, values_field, precision=precise_mode)
    return jnp.einsum('kz,abxyz->abxyk', cas_values, values_field, precision=precise_mode)


def reference(orbitals, offsets):
    cas_values = cas_table(NG)
    kernel = screened_kernel(NG)
    blocks_all = orbitals.reshape(N_BLK, OB, NG, NG, NG)
    cycle_index = jnp.arange(N_BLK, dtype=jnp.int32)
    accumulator = jnp.zeros_like(blocks_all)

    def one_block(pair_items):
        own_block, vis_block = pair_items
        density = own_block[:, None] * vis_block[None, :]
        potential = hartley_cube(hartley_cube(density, cas_values) * kernel, cas_values) / float(NG ** 3)
        return jnp.sum(potential * vis_block[None, :], axis=1)

    for replica in range(N_REP):
        for step_index in range(STEPS):
            source_block = (cycle_index - offsets[replica] - step_index) % N_BLK
            visiting = jnp.take(blocks_all, source_block.astype(jnp.int32), axis=0)
            accumulator = accumulator + lax.map(one_block, (blocks_all, visiting))
    exchanged = accumulator.reshape(NORB, NG ** 3)
    margin = lax.dot_general(orbitals, exchanged, (((1,), (1,)), ((), ())), precision=precise_mode) / float(NG ** 3)
    return exchanged, margin
```

```python
import jax
import jax.numpy as jnp
from jax import lax
from jax.sharding import PartitionSpec as P

NG = 64


precise_mode = lax.Precision.HIGHEST
solve_mode = lax.Precision.HIGH
STEPS = 3
screen_scale = 0.05


def passed_along(block, axis, distance):
    devices = range(lax.axis_size(axis))
    route = [((i - distance) % len(devices), i) for i in devices]
    return lax.ppermute(block, axis, route)


def cas_table(grid_points):
    grid_index = jnp.arange(grid_points, dtype=jnp.int32)
    product = grid_index[:, None] * grid_index[None, :] % grid_points
    phase_angle = 2.0 * jnp.pi / grid_points * product.astype(jnp.float32)
    return jnp.cos(phase_angle) + jnp.sin(phase_angle)


def screened_kernel(grid_points):
    grid_index = jnp.arange(grid_points, dtype=jnp.int32)
    folded = jnp.where(grid_index <= grid_points // 2, grid_index, grid_index - grid_points).astype(
        jnp.float32
    )
    squares = folded * folded
    k_squared = squares[:, None, None] + squares[None, :, None] + squares[None, None, :]
    safe_square = jnp.maximum(k_squared, 1.0)
    screened = (
        4.0
        * jnp.pi
        / (screen_scale * safe_square)
        * (1.0 - jnp.exp(-screen_scale * safe_square / (4.0 * jnp.pi)))
    )
    return jnp.where(k_squared > 0.5, screened, jnp.ones_like(screened))


def transform(values_field, cas_values, cas_paired):
    batch_size = values_field.shape[0]
    grid_points = values_field.shape[1]
    values_field = jnp.einsum(
        "kx,pxq->pkq",
        cas_values,
        values_field.reshape(batch_size, grid_points, grid_points * grid_points),
        precision=solve_mode,
    )
    values_field = jnp.einsum(
        "ky,ayz->akz",
        cas_values,
        values_field.reshape(batch_size * grid_points, grid_points, grid_points),
        precision=solve_mode,
    )
    values_field = jnp.dot(
        values_field.reshape(batch_size * grid_points * grid_points // 2, 2 * grid_points),
        cas_paired,
        precision=solve_mode,
    )
    return values_field.reshape(batch_size, grid_points, grid_points, grid_points)


def cycle_term(own_block, visiting, cas_values, cas_paired, kernel):
    grid_points = kernel.shape[0]
    block_rows = own_block.shape[0]
    density = (own_block[:, None, :] * visiting[None, :, :]).reshape(
        block_rows * block_rows, grid_points, grid_points, grid_points
    )
    spectrum = transform(density, cas_values, cas_paired) * kernel[None]
    potential = transform(spectrum, cas_values, cas_paired).reshape(
        block_rows, block_rows, grid_points**3
    ) / float(grid_points**3)
    return jnp.sum(potential * visiting[None, :, :], axis=1)


def position_block(orbital_block, amount):
    bit_count = (lax.axis_size("blk") - 1).bit_length()
    for bit_level in range(bit_count):
        moved_block = passed_along(orbital_block, "blk", 1 << bit_level)
        orbital_block = jnp.where(amount // (1 << bit_level) % 2 == 1, moved_block, orbital_block)
    return orbital_block


def finish(accumulator, orbitals):
    replica = lax.axis_index("rep")
    exchanged = lax.psum_scatter(accumulator, "rep", scatter_dimension=1, tiled=True)
    quarter_cells = exchanged.shape[1]
    quarter = lax.dynamic_slice_in_dim(orbitals, replica * quarter_cells, quarter_cells, 1)
    slab_orbitals, slab_exchanged = (
        lax.all_to_all(quarter, "blk", split_axis=1, concat_axis=0, tiled=True),
        lax.all_to_all(exchanged, "blk", split_axis=1, concat_axis=0, tiled=True),
    )
    partial_value = lax.dot_general(
        slab_orbitals, slab_exchanged, (((1,), (1,)), ((), ())), precision=precise_mode
    ) / float(NG**3)
    gram_rows = lax.psum_scatter(partial_value, "blk", scatter_dimension=0, tiled=True)
    margin = lax.psum(gram_rows, "rep")
    return (exchanged, margin)


def local_steps(orbitals, offsets):
    cas_values = cas_table(NG)
    cas_paired = jnp.kron(jnp.eye(2, dtype=jnp.float32), cas_values)
    kernel = screened_kernel(NG)
    cycle_size = lax.axis_size("blk")
    replica = lax.axis_index("rep")
    start_block = offsets[replica]
    first_visit = position_block(orbitals, (start_block + 1) % cycle_size)
    behind = passed_along(first_visit, "blk", -1)
    accumulator = cycle_term(orbitals, first_visit, cas_values, cas_paired, kernel)
    ahead_block = passed_along(first_visit, "blk", 1)
    accumulator = accumulator + cycle_term(orbitals, ahead_block, cas_values, cas_paired, kernel)
    accumulator = accumulator + cycle_term(orbitals, behind, cas_values, cas_paired, kernel)
    return finish(accumulator, orbitals)


def distance_counts(offsets, cycle_size):
    met = (offsets[:, None] + jnp.arange(STEPS, dtype=jnp.int32)[None, :]) % cycle_size
    distances = jnp.arange(cycle_size, dtype=jnp.int32)
    return jnp.sum((met[None] == distances[:, None, None]).astype(jnp.float32), axis=(1, 2))


def local_distances(orbitals, offsets):
    cycle_size = lax.axis_size("blk")
    replicas = lax.axis_size("rep")
    counts = distance_counts(offsets, cycle_size)
    cas_values = cas_table(NG)
    cas_paired = jnp.kron(jnp.eye(2, dtype=jnp.float32), cas_values)
    kernel = screened_kernel(NG)
    route = [
        (b * replicas + d, (b + d) % cycle_size * replicas + d)
        for b in range(cycle_size)
        for d in range(replicas)
    ]
    visiting = lax.ppermute(orbitals, ("blk", "rep"), route)
    weight = counts[lax.axis_index("rep")]
    accumulator = weight * cycle_term(orbitals, visiting, cas_values, cas_paired, kernel)
    return finish(accumulator, orbitals)


def solution(mesh):
    placed = (P(("groups", "blk"), None), P("groups"))
    one_each = mesh.shape["blk"] == mesh.shape["rep"]
    local = local_distances if one_each else local_steps
    return jax.shard_map(
        local,
        mesh=mesh,
        in_specs=placed,
        out_specs=(P(("groups", "blk"), "rep"), P(("groups", "blk"), None)),
        check_vma=False,
    )
```

```python
import functools

import jax
import jax.numpy as jnp
import numpy as np
from jax import lax
from jax.experimental import pallas as pl
from jax.experimental.pallas import tpu as pltpu
from jax.sharding import PartitionSpec as P

NG = 64


precise_mode = lax.Precision.HIGHEST
solve_mode = lax.Precision.HIGH
STEPS = 3
screen_scale = 0.05


def passed_along(block, axis, distance):
    devices = range(lax.axis_size(axis))
    route = [((i - distance) % len(devices), i) for i in devices]
    return lax.ppermute(block, axis, route)


def cas_table(grid_points):
    grid_index = jnp.arange(grid_points, dtype=jnp.int32)
    product = grid_index[:, None] * grid_index[None, :] % grid_points
    phase_angle = 2.0 * jnp.pi / grid_points * product.astype(jnp.float32)
    return jnp.cos(phase_angle) + jnp.sin(phase_angle)


def screened_kernel(grid_points):
    grid_index = jnp.arange(grid_points, dtype=jnp.int32)
    folded = jnp.where(grid_index <= grid_points // 2, grid_index, grid_index - grid_points).astype(
        jnp.float32
    )
    squares = folded * folded
    k_squared = squares[:, None, None] + squares[None, :, None] + squares[None, None, :]
    safe_square = jnp.maximum(k_squared, 1.0)
    screened = (
        4.0
        * jnp.pi
        / (screen_scale * safe_square)
        * (1.0 - jnp.exp(-screen_scale * safe_square / (4.0 * jnp.pi)))
    )
    return jnp.where(k_squared > 0.5, screened, jnp.ones_like(screened))


def transform(values_field, cas_values, cas_paired):
    batch_size = values_field.shape[0]
    grid_points = values_field.shape[1]
    values_field = jnp.einsum(
        "kx,pxq->pkq",
        cas_values,
        values_field.reshape(batch_size, grid_points, grid_points * grid_points),
        precision=solve_mode,
    )
    values_field = jnp.einsum(
        "ky,ayz->akz",
        cas_values,
        values_field.reshape(batch_size * grid_points, grid_points, grid_points),
        precision=solve_mode,
    )
    values_field = jnp.dot(
        values_field.reshape(batch_size * grid_points * grid_points // 2, 2 * grid_points),
        cas_paired,
        precision=solve_mode,
    )
    return values_field.reshape(batch_size, grid_points, grid_points, grid_points)


def cycle_term(own_block, visiting, cas_values, cas_paired, kernel):
    grid_points = kernel.shape[0]
    block_rows = own_block.shape[0]
    density = (own_block[:, None, :] * visiting[None, :, :]).reshape(
        block_rows * block_rows, grid_points, grid_points, grid_points
    )
    spectrum = transform(density, cas_values, cas_paired) * kernel[None]
    potential = transform(spectrum, cas_values, cas_paired).reshape(
        block_rows, block_rows, grid_points**3
    ) / float(grid_points**3)
    return jnp.sum(potential * visiting[None, :, :], axis=1)


def position_block(orbital_block, amount):
    bit_count = (lax.axis_size("blk") - 1).bit_length()
    for bit_level in range(bit_count):
        moved_block = passed_along(orbital_block, "blk", 1 << bit_level)
        orbital_block = jnp.where(amount // (1 << bit_level) % 2 == 1, moved_block, orbital_block)
    return orbital_block


def finish(accumulator, orbitals):
    replica = lax.axis_index("rep")
    exchanged = lax.psum_scatter(accumulator, "rep", scatter_dimension=1, tiled=True)
    quarter_cells = exchanged.shape[1]
    quarter = lax.dynamic_slice_in_dim(orbitals, replica * quarter_cells, quarter_cells, 1)
    slab_orbitals, slab_exchanged = (
        lax.all_to_all(quarter, "blk", split_axis=1, concat_axis=0, tiled=True),
        lax.all_to_all(exchanged, "blk", split_axis=1, concat_axis=0, tiled=True),
    )
    partial_value = lax.dot_general(
        slab_orbitals, slab_exchanged, (((1,), (1,)), ((), ())), precision=precise_mode
    ) / float(NG**3)
    gram_rows = lax.psum_scatter(partial_value, "blk", scatter_dimension=0, tiled=True)
    margin = lax.psum(gram_rows, "rep")
    return (exchanged, margin)


def local_steps(orbitals, offsets):
    cas_values = cas_table(NG)
    cas_paired = jnp.kron(jnp.eye(2, dtype=jnp.float32), cas_values)
    kernel = screened_kernel(NG)
    cycle_size = lax.axis_size("blk")
    replica = lax.axis_index("rep")
    start_block = offsets[replica]
    first_visit = position_block(orbitals, (start_block + 1) % cycle_size)
    behind = passed_along(first_visit, "blk", -1)
    accumulator = cycle_term(orbitals, first_visit, cas_values, cas_paired, kernel)
    ahead_block = passed_along(first_visit, "blk", 1)
    accumulator = accumulator + cycle_term(orbitals, ahead_block, cas_values, cas_paired, kernel)
    accumulator = accumulator + cycle_term(orbitals, behind, cas_values, cas_paired, kernel)
    return finish(accumulator, orbitals)


MESH = pl.DeviceIdType.MESH
LANES = 128


def two_halves(table):
    high = table.astype(jnp.bfloat16)
    low = (table - high.astype(np.float64)).astype(jnp.bfloat16)
    return high, low


def cas_tables(grid_points):
    index = np.arange(grid_points)
    angle = 2.0 * np.pi / grid_points * (np.outer(index, index) % grid_points)
    cas = np.cos(angle) + np.sin(angle)
    high, low = two_halves(np.kron(np.eye(2), cas))
    last_main = np.concatenate([high, high], axis=0)
    blocks = [cas[k::2, y::2] for k in range(2) for y in range(2)]
    y_high, y_low = two_halves(np.concatenate(blocks, axis=0))
    middle = np.concatenate([y_high, y_high, y_low], axis=1)
    x_high, x_low = two_halves(cas)
    first = np.concatenate([x_high, x_high, x_low], axis=1)
    return [jnp.asarray(t) for t in (last_main, low, middle, first)]


def split(values):
    high = values.astype(jnp.bfloat16)
    return high, (values - high.astype(jnp.float32)).astype(jnp.bfloat16)


def dot(a, b):
    return jnp.dot(a, b, preferred_element_type=jnp.float32)


def last_axis(values, main_ref, low_ref):
    high, low = split(values)
    return dot(jnp.concatenate([high, low], axis=1), main_ref[...]) + dot(high, low_ref[...])


def middle_axis(pair, middle_ref):
    half = pair.shape[0]
    high, low = split(pair)
    terms = dot(middle_ref[...], jnp.concatenate([high, low, high], axis=0))
    lane = lax.broadcasted_iota(jnp.int32, (half, pair.shape[1]), 1) % LANES
    first = lane < LANES // 2
    t = [terms[i * half : (i + 1) * half] for i in range(4)]
    straight = jnp.where(first, t[0], t[3])
    crossed = jnp.where(first, t[2], t[1])
    return [
        straight[:, at : at + LANES] + pltpu.roll(crossed[:, at : at + LANES], LANES // 2, 1)
        for at in (0, LANES)
    ]


def first_axis(values, first_ref):
    high, low = split(values)
    return dot(first_ref[...], jnp.concatenate([high, low, high], axis=0))


def exchange_kernel(
    n,
    pieces,
    group,
    offsets_ref,
    psi_ref,
    main_ref,
    low_ref,
    middle_ref,
    first_ref,
    exchanged_ref,
    margin_ref,
    parts,
    met,
    field,
    table,
    outgoing,
    incoming,
    my_rows,
    all_rows,
    part_sent,
    part_got,
    met_sent,
    met_got,
    local_sem,
    term_sent,
    term_got,
    rows_sent,
    rows_got,
):
    b = lax.axis_index("blk")
    r = lax.axis_index("rep")
    rows = psi_ref.shape[0]
    quarter = rows // n
    piece = quarter // pieces
    plane = NG * NG // LANES
    me = b * n + r

    def device(at):
        return {"blk": at // n, "rep": at % n}

    barrier = pltpu.get_barrier_semaphore()
    for j in range(1, n * n):
        pl.semaphore_signal(
            barrier, inc=1, device_id=device((me + j) % (n * n)), device_id_type=MESH
        )
    pl.semaphore_wait(barrier, n * n - 1)

    def part_copy(c, p, to):
        start = pl.multiple_of(r * quarter + p * piece, 8)
        return pltpu.make_async_remote_copy(
            src_ref=psi_ref.at[pl.ds(start, piece)],
            dst_ref=parts.at[c, pl.ds(p * piece, piece)],
            send_sem=part_sent.at[to, p],
            recv_sem=part_got.at[c, p],
            device_id={"blk": to, "rep": r},
            device_id_type=MESH,
        )

    for p in range(pieces):
        for j in range(1, n):
            part_copy(b, p, (b + j) % n).start()

    own_copy = pltpu.make_async_copy(psi_ref, met, local_sem.at[0])

    @pl.when(r == 0)
    def _():
        own_copy.start()

    def folded(index):
        return jnp.where(index <= NG // 2, index, index - NG).astype(jnp.float32)

    lane = lax.broadcasted_iota(jnp.int32, (NG, LANES), 1)
    kx = folded(lax.broadcasted_iota(jnp.int32, (NG, LANES), 0))
    kz = folded(lane % NG)
    base = kx * kx + kz * kz

    def fill(k, _):
        ky = folded(2 * k + lane // NG)
        k_squared = base + ky * ky
        safe = jnp.maximum(k_squared, 1.0)
        scaled = screen_scale * safe / (4.0 * jnp.pi)
        screened = (1.0 - jnp.exp(-scaled)) / scaled
        start = pl.multiple_of(k * NG, NG)
        table[pl.ds(start, NG), :] = jnp.where(k_squared > 0.5, screened, 1.0)
        return 0

    lax.fori_loop(0, plane, fill, 0)

    def met_copy(c, p, slot, d):
        return pltpu.make_async_remote_copy(
            src_ref=parts.at[c, pl.ds(p * piece, piece)],
            dst_ref=met.at[pl.ds(pl.multiple_of(slot * quarter + p * piece, 8), piece)],
            send_sem=met_sent.at[d, p],
            recv_sem=met_got.at[slot, p],
            device_id={"blk": b, "rep": d},
            device_id_type=MESH,
        )

    def met_local(c, p):
        return pltpu.make_async_copy(
            parts.at[c, pl.ds(p * piece, piece)],
            met.at[pl.ds(pl.multiple_of(r * quarter + p * piece, 8), piece)],
            local_sem.at[1 + p],
        )

    order = sorted(range(1, n), key=lambda j: min(j, n - j))
    for p in range(pieces):
        for j in order:
            c = (b + j) % n
            d = (n - j) % n
            part_copy(c, p, c).wait_recv()

            @pl.when(d == r)
            def _():
                met_local(c, p).start()

            @pl.when(d != r)
            def _():
                met_copy(c, p, r, d).start()

    count = jnp.float32(0.0)
    for other in range(n):
        for step in range(STEPS):
            count = count + jnp.where((offsets_ref[other] + step) % n == r, 1.0, 0.0)
    scale = count / float(NG**3)

    batch = 4

    def forward(start):
        density = psi_ref[pl.ds(start, batch * plane), :] * met[pl.ds(start, batch * plane), :]
        along_z = last_axis(density, main_ref, low_ref)
        for i in range(0, batch, 2):
            pair = jnp.concatenate(
                [
                    along_z[i * plane : (i + 1) * plane],
                    along_z[(i + 1) * plane : (i + 2) * plane],
                ],
                axis=1,
            )
            for k, out in enumerate(middle_axis(pair, middle_ref)):
                at = pl.multiple_of(start + (i + k) * plane, plane)
                field[pl.ds(at, plane), :] = out

    @pl.when(r == 0)
    def _():
        own_copy.wait()

    steps = piece // (batch * plane)
    for j in range(n):
        slot = (r + j) % n
        for p in range(pieces):
            if j == 0:

                @pl.when(r != 0)
                def _():
                    met_local(b, p).wait()

            else:

                @pl.when(r != 0)
                def _():
                    met_copy(b, p, slot, slot).wait_recv()

            def forward_step(i, _):
                start = slot * quarter + p * piece + i * (batch * plane)
                forward(pl.multiple_of(start, batch * plane))
                return 0

            lax.fori_loop(0, steps, forward_step, 0)

    def across(i, _):
        k = 2 * i
        both = jnp.concatenate(
            [
                field[pl.ds(k, NG, stride=plane), :],
                field[pl.ds(k + 1, NG, stride=plane), :],
            ],
            axis=1,
        )
        at = pl.multiple_of(k * NG, NG)
        factor = jnp.concatenate(
            [table[pl.ds(at, NG), :], table[pl.ds(at + NG, NG), :]], axis=1
        )
        back = first_axis(first_axis(both, first_ref) * factor, first_ref)
        field[pl.ds(k, NG, stride=plane), :] = back[:, :LANES]
        field[pl.ds(k + 1, NG, stride=plane), :] = back[:, LANES:]
        return 0

    lax.fori_loop(0, plane // 2, across, 0)

    def backward(slot, i):
        start = pl.multiple_of(slot * quarter + i * (batch * plane), batch * plane)
        values = field[pl.ds(start, batch * plane), :]
        turned = []
        for k in range(0, batch, 2):
            pair = jnp.concatenate(
                [
                    values[k * plane : (k + 1) * plane],
                    values[(k + 1) * plane : (k + 2) * plane],
                ],
                axis=1,
            )
            turned += middle_axis(pair, middle_ref)
        potential = last_axis(jnp.concatenate(turned, axis=0), main_ref, low_ref)
        return potential * (met[pl.ds(start, batch * plane), :] * scale)

    def term_copy(at, to, source):
        return pltpu.make_async_remote_copy(
            src_ref=outgoing.at[at],
            dst_ref=incoming.at[source],
            send_sem=term_sent.at[at],
            recv_sem=term_got.at[source],
            device_id={"blk": b, "rep": to},
            device_id_type=MESH,
        )

    away = list(range(n - 1, 0, -1))
    for at, j in enumerate(away):
        slot = (r + j) % n

        def send_step(i, _):
            here = pl.multiple_of(i * (batch * plane), batch * plane)
            outgoing[at, pl.ds(here, batch * plane), :] = backward(slot, i)
            return 0

        lax.fori_loop(0, quarter // (batch * plane), send_step, 0)
        term_copy(at, slot, r).start()

    def own_step(i, _):
        here = pl.multiple_of(i * (batch * plane), batch * plane)
        exchanged_ref[pl.ds(here, batch * plane), :] = backward(r, i)
        return 0

    lax.fori_loop(0, quarter // (batch * plane), own_step, 0)
    for at, j in enumerate(away):
        source = (r + n - j) % n
        term_copy(at, source, source).wait_recv()

    def total_step(i, sums):
        here = pl.multiple_of(i * 64, 64)
        total = exchanged_ref[pl.ds(here, 64), :]
        for j in range(1, n):
            total = total + incoming[(r + j) % n, pl.ds(here, 64), :]
        exchanged_ref[pl.ds(here, 64), :] = total
        mine = psi_ref[pl.ds(pl.multiple_of(r * quarter + i * 64, 64), 64), :]
        found = [jnp.sum((mine * total).reshape(8, 8, LANES), axis=0)]
        for j in range(1, n):
            seen = parts[(b + j) % n, pl.ds(here, 64), :]
            found.append(jnp.sum((seen * total).reshape(8, 8, LANES), axis=0))
        return tuple(s + f for s, f in zip(sums, found))

    zeros = jnp.zeros((8, LANES), jnp.float32)
    sums = lax.fori_loop(0, quarter // 64, total_step, (zeros,) * n)
    sublane = lax.broadcasted_iota(jnp.int32, (8, LANES), 0)
    packed = jnp.zeros((8, LANES), jnp.float32)
    for j in range(n):
        line = jnp.sum(sums[j], axis=0, keepdims=True)
        packed = packed + jnp.where(sublane == (b + j) % n, line, 0.0)
    my_rows[...] = packed

    def rows_copy(to, source, j):
        return pltpu.make_async_remote_copy(
            src_ref=my_rows,
            dst_ref=all_rows.at[source],
            send_sem=rows_sent.at[j],
            recv_sem=rows_got.at[source],
            device_id=device(to),
            device_id_type=MESH,
        )

    for j in range(1, n * n):
        rows_copy((me + j) % (n * n), me, j).start()
    all_rows[me] = packed
    for j in range(1, n * n):
        source = (me + j) % (n * n)
        rows_copy(source, source, j).wait_recv()

    wanted = sublane == b
    place = lax.broadcasted_iota(jnp.int32, (1, n), 1)
    answer = jnp.zeros((1, n), jnp.float32)
    for c in range(n):
        whole = all_rows[c * n]
        for k in range(1, n):
            whole = whole + all_rows[c * n + k]
        value = jnp.sum(jnp.where(wanted, whole, 0.0)) / float(NG**3)
        answer = jnp.where(place == c, value, answer)
    margin_ref[...] = answer

    for j in range(1, n * n):
        rows_copy((me + j) % (n * n), me, j).wait_send()
    for at, j in enumerate(away):
        term_copy(at, (r + j) % n, r).wait_send()
    for p in range(pieces):
        for j in range(1, n):
            part_copy(b, p, (b + j) % n).wait_send()
            c = (b + j) % n
            d = (n - j) % n

            @pl.when(d != r)
            def _():
                met_copy(c, p, r, d).wait_send()


def local_distances(orbitals, offsets):
    n = lax.axis_size("blk")
    pieces = 2
    rows = orbitals.shape[1] // LANES
    quarter = rows // n
    tables = cas_tables(NG)
    f32 = jnp.float32
    vmem = pl.BlockSpec(memory_space=pltpu.VMEM)
    exchanged, margin = pl.pallas_call(
        functools.partial(exchange_kernel, n, pieces, None),
        out_shape=(
            jax.ShapeDtypeStruct((quarter, LANES), f32),
            jax.ShapeDtypeStruct((1, n), f32),
        ),
        in_specs=[pl.BlockSpec(memory_space=pltpu.SMEM)] + [vmem] * 5,
        out_specs=(vmem, vmem),
        scratch_shapes=[
            pltpu.VMEM((n, quarter, LANES), f32),
            pltpu.VMEM((rows, LANES), f32),
            pltpu.VMEM((rows, LANES), f32),
            pltpu.VMEM((rows, LANES), f32),
            pltpu.VMEM((n - 1, quarter, LANES), f32),
            pltpu.VMEM((n, quarter, LANES), f32),
            pltpu.VMEM((8, LANES), f32),
            pltpu.VMEM((n * n, 8, LANES), f32),
            pltpu.SemaphoreType.DMA((n, pieces)),
            pltpu.SemaphoreType.DMA((n, pieces)),
            pltpu.SemaphoreType.DMA((n, pieces)),
            pltpu.SemaphoreType.DMA((n, pieces)),
            pltpu.SemaphoreType.DMA((1 + pieces,)),
            pltpu.SemaphoreType.DMA((n,)),
            pltpu.SemaphoreType.DMA((n,)),
            pltpu.SemaphoreType.DMA((n * n,)),
            pltpu.SemaphoreType.DMA((n * n,)),
        ],
        compiler_params=pltpu.CompilerParams(collective_id=0, has_side_effects=True),
    )(offsets, orbitals.reshape(rows, LANES), *tables)
    return exchanged.reshape(1, quarter * LANES), margin


def solution(mesh):
    placed = (P(("groups", "blk"), None), P("groups"))
    one_each = mesh.shape["blk"] == mesh.shape["rep"]
    local = local_distances if one_each else local_steps
    return jax.shard_map(
        local,
        mesh=mesh,
        in_specs=placed,
        out_specs=(P(("groups", "blk"), "rep"), P(("groups", "blk"), None)),
        check_vma=False,
    )
```

```python
import functools

import jax
import jax.numpy as jnp
import numpy as np
from jax import lax
from jax.experimental import pallas as pl
from jax.experimental.pallas import tpu as pltpu
from jax.sharding import PartitionSpec as P

NG = 64


precise_mode = lax.Precision.HIGHEST
solve_mode = lax.Precision.HIGH
STEPS = 3
screen_scale = 0.05


def passed_along(block, axis, distance):
    devices = range(lax.axis_size(axis))
    route = [((i - distance) % len(devices), i) for i in devices]
    return lax.ppermute(block, axis, route)


def cas_table(grid_points):
    grid_index = jnp.arange(grid_points, dtype=jnp.int32)
    product = grid_index[:, None] * grid_index[None, :] % grid_points
    phase_angle = 2.0 * jnp.pi / grid_points * product.astype(jnp.float32)
    return jnp.cos(phase_angle) + jnp.sin(phase_angle)


def screened_kernel(grid_points):
    grid_index = jnp.arange(grid_points, dtype=jnp.int32)
    folded = jnp.where(grid_index <= grid_points // 2, grid_index, grid_index - grid_points).astype(
        jnp.float32
    )
    squares = folded * folded
    k_squared = squares[:, None, None] + squares[None, :, None] + squares[None, None, :]
    safe_square = jnp.maximum(k_squared, 1.0)
    screened = (
        4.0
        * jnp.pi
        / (screen_scale * safe_square)
        * (1.0 - jnp.exp(-screen_scale * safe_square / (4.0 * jnp.pi)))
    )
    return jnp.where(k_squared > 0.5, screened, jnp.ones_like(screened))


def transform(values_field, cas_values, cas_paired):
    batch_size = values_field.shape[0]
    grid_points = values_field.shape[1]
    values_field = jnp.einsum(
        "kx,pxq->pkq",
        cas_values,
        values_field.reshape(batch_size, grid_points, grid_points * grid_points),
        precision=solve_mode,
    )
    values_field = jnp.einsum(
        "ky,ayz->akz",
        cas_values,
        values_field.reshape(batch_size * grid_points, grid_points, grid_points),
        precision=solve_mode,
    )
    values_field = jnp.dot(
        values_field.reshape(batch_size * grid_points * grid_points // 2, 2 * grid_points),
        cas_paired,
        precision=solve_mode,
    )
    return values_field.reshape(batch_size, grid_points, grid_points, grid_points)


def cycle_term(own_block, visiting, cas_values, cas_paired, kernel):
    grid_points = kernel.shape[0]
    block_rows = own_block.shape[0]
    density = (own_block[:, None, :] * visiting[None, :, :]).reshape(
        block_rows * block_rows, grid_points, grid_points, grid_points
    )
    spectrum = transform(density, cas_values, cas_paired) * kernel[None]
    potential = transform(spectrum, cas_values, cas_paired).reshape(
        block_rows, block_rows, grid_points**3
    ) / float(grid_points**3)
    return jnp.sum(potential * visiting[None, :, :], axis=1)


def position_block(orbital_block, amount):
    bit_count = (lax.axis_size("blk") - 1).bit_length()
    for bit_level in range(bit_count):
        moved_block = passed_along(orbital_block, "blk", 1 << bit_level)
        orbital_block = jnp.where(amount // (1 << bit_level) % 2 == 1, moved_block, orbital_block)
    return orbital_block


def finish(accumulator, orbitals):
    replica = lax.axis_index("rep")
    exchanged = lax.psum_scatter(accumulator, "rep", scatter_dimension=1, tiled=True)
    quarter_cells = exchanged.shape[1]
    quarter = lax.dynamic_slice_in_dim(orbitals, replica * quarter_cells, quarter_cells, 1)
    slab_orbitals, slab_exchanged = (
        lax.all_to_all(quarter, "blk", split_axis=1, concat_axis=0, tiled=True),
        lax.all_to_all(exchanged, "blk", split_axis=1, concat_axis=0, tiled=True),
    )
    partial_value = lax.dot_general(
        slab_orbitals, slab_exchanged, (((1,), (1,)), ((), ())), precision=precise_mode
    ) / float(NG**3)
    gram_rows = lax.psum_scatter(partial_value, "blk", scatter_dimension=0, tiled=True)
    margin = lax.psum(gram_rows, "rep")
    return (exchanged, margin)


def local_steps(orbitals, offsets):
    cas_values = cas_table(NG)
    cas_paired = jnp.kron(jnp.eye(2, dtype=jnp.float32), cas_values)
    kernel = screened_kernel(NG)
    cycle_size = lax.axis_size("blk")
    replica = lax.axis_index("rep")
    start_block = offsets[replica]
    first_visit = position_block(orbitals, (start_block + 1) % cycle_size)
    behind = passed_along(first_visit, "blk", -1)
    accumulator = cycle_term(orbitals, first_visit, cas_values, cas_paired, kernel)
    ahead_block = passed_along(first_visit, "blk", 1)
    accumulator = accumulator + cycle_term(orbitals, ahead_block, cas_values, cas_paired, kernel)
    accumulator = accumulator + cycle_term(orbitals, behind, cas_values, cas_paired, kernel)
    return finish(accumulator, orbitals)


MESH = pl.DeviceIdType.MESH
LANES = 128


def two_halves(table):
    high = table.astype(jnp.bfloat16)
    low = (table - high.astype(np.float64)).astype(jnp.bfloat16)
    return high, low


def cas_tables(grid_points):
    index = np.arange(grid_points)
    angle = 2.0 * np.pi / grid_points * (np.outer(index, index) % grid_points)
    cas = np.cos(angle) + np.sin(angle)
    high, low = two_halves(np.kron(np.eye(2), cas))
    last_main = np.concatenate([high, high], axis=0)
    blocks = [cas[k::2, y::2] for k in range(2) for y in range(2)]
    y_high, y_low = two_halves(np.concatenate(blocks, axis=0))
    middle = np.concatenate([y_high, y_high, y_low], axis=1)
    x_high, x_low = two_halves(cas)
    first = np.concatenate([x_high, x_high, x_low], axis=1)
    return [jnp.asarray(t) for t in (last_main, low, middle, first)]


def split(values):
    high = values.astype(jnp.bfloat16)
    return high, (values - high.astype(jnp.float32)).astype(jnp.bfloat16)


def dot(a, b):
    return jnp.dot(a, b, preferred_element_type=jnp.float32)


def last_axis(values, main_ref, low_ref):
    high, low = split(values)
    return dot(jnp.concatenate([high, low], axis=1), main_ref[...]) + dot(high, low_ref[...])


def middle_axis(pair, middle_ref):
    half = pair.shape[0]
    high, low = split(pair)
    terms = dot(middle_ref[...], jnp.concatenate([high, low, high], axis=0))
    lane = lax.broadcasted_iota(jnp.int32, (half, pair.shape[1]), 1) % LANES
    first = lane < LANES // 2
    t = [terms[i * half : (i + 1) * half] for i in range(4)]
    straight = jnp.where(first, t[0], t[3])
    crossed = jnp.where(first, t[2], t[1])
    return [
        straight[:, at : at + LANES] + pltpu.roll(crossed[:, at : at + LANES], LANES // 2, 1)
        for at in (0, LANES)
    ]


def first_axis(values, first_ref):
    high, low = split(values)
    return dot(first_ref[...], jnp.concatenate([high, low, high], axis=0))


def exchange_kernel(
    n,
    pieces,
    offsets_ref,
    psi_ref,
    main_ref,
    low_ref,
    middle_ref,
    first_ref,
    exchanged_ref,
    margin_ref,
    parts,
    met,
    field,
    table,
    pair_out,
    pair_in,
    cross_out,
    cross_in,
    my_rows,
    all_rows,
    up_sent,
    down_sent,
    part_got,
    met_sent,
    met_got,
    local_sem,
    pair_sent,
    pair_got,
    cross_sent,
    cross_got,
    rows_sent,
    rows_got,
):
    b = lax.axis_index("blk")
    r = lax.axis_index("rep")
    rows = psi_ref.shape[0]
    quarter = rows // n
    piece = quarter // pieces
    plane = NG * NG // LANES
    batch = piece // plane
    me = b * n + r
    chips = n // 2
    chip = r // 2
    side = r % 2
    partner = r + 1 - 2 * side

    def device(at):
        return {"blk": at // n, "rep": at % n}

    barrier = pltpu.get_barrier_semaphore()
    for j in range(1, n * n):
        pl.semaphore_signal(
            barrier, inc=1, device_id=device((me + j) % (n * n)), device_id_type=MESH
        )
    pl.semaphore_wait(barrier, n * n - 1)

    def at_piece(p):
        return pl.ds(pl.multiple_of(p * piece, 8), piece)

    def quarter_piece(slot, p):
        return pl.ds(pl.multiple_of(slot * quarter + p * piece, 8), piece)

    def part_copy(source, c, p, to, sent):
        return pltpu.make_async_remote_copy(
            src_ref=source,
            dst_ref=parts.at[c, at_piece(p)],
            send_sem=sent.at[c, p],
            recv_sem=part_got.at[c, p],
            device_id={"blk": to, "rep": r},
            device_id_type=MESH,
        )

    def own_copy(p, to, sent):
        return part_copy(psi_ref.at[quarter_piece(r, p)], b, p, to, sent)

    def relay_copy(c, p, to, sent):
        return part_copy(parts.at[c, at_piece(p)], c, p, to, sent)

    @pl.when(b < n - 1)
    def _():
        for p in range(pieces):
            own_copy(p, b + 1, up_sent).start()

    @pl.when(b > 0)
    def _():
        for p in range(pieces):
            own_copy(p, b - 1, down_sent).start()

    whole_copy = pltpu.make_async_copy(psi_ref, met, local_sem.at[0])

    @pl.when(r == 0)
    def _():
        whole_copy.start()

    def folded(index):
        return jnp.where(index <= NG // 2, index, index - NG).astype(jnp.float32)

    lane = lax.broadcasted_iota(jnp.int32, (NG, LANES), 1)
    kx = folded(lax.broadcasted_iota(jnp.int32, (NG, LANES), 0))
    kz = folded(lane % NG)
    base = kx * kx + kz * kz

    def fill(k):
        ky = folded(2 * k + lane // NG)
        k_squared = base + ky * ky
        safe = jnp.maximum(k_squared, 1.0)
        scaled = screen_scale * safe / (4.0 * jnp.pi)
        screened = (1.0 - jnp.exp(-scaled)) / scaled
        start = pl.multiple_of(k * NG, NG)
        table[pl.ds(start, NG), :] = jnp.where(k_squared > 0.5, screened, 1.0)

    def met_copy(c, p, slot, d):
        return pltpu.make_async_remote_copy(
            src_ref=parts.at[c, at_piece(p)],
            dst_ref=met.at[quarter_piece(slot, p)],
            send_sem=met_sent.at[d, p],
            recv_sem=met_got.at[slot, p],
            device_id={"blk": b, "rep": d},
            device_id_type=MESH,
        )

    def met_local(c, p):
        return pltpu.make_async_copy(
            parts.at[c, at_piece(p)], met.at[quarter_piece(r, p)], local_sem.at[1 + p]
        )

    def planes_of(values):
        return [values[i * plane : (i + 1) * plane] for i in range(batch)]

    def middle_all(values):
        whole = planes_of(values)
        turned = []
        for i in range(0, batch, 2):
            pair = jnp.concatenate([whole[i], whole[i + 1]], axis=1)
            turned += middle_axis(pair, middle_ref)
        return jnp.concatenate(turned, axis=0)

    def forward(slot, p):
        here = quarter_piece(slot, p)
        density = psi_ref[here, :] * met[here, :]
        field[here, :] = middle_all(last_axis(density, main_ref, low_ref))

    def forward_met(p):
        met_local(b, p).wait()
        forward(r, p)

        def one(j, _):
            slot = (r + j) % n
            met_copy(b, p, slot, slot).wait_recv()
            forward(slot, p)
            return 0

        lax.fori_loop(1, n, one, 0)

    count = (n - 1) * pieces
    fills = pl.cdiv(plane, count)
    wanted_block = (b - r + n) % n
    wanted_steps = jnp.maximum(wanted_block - b, b - wanted_block)

    @pl.when(r == 0)
    def _():
        whole_copy.wait()

        def one(t, _):
            forward(t // pieces, t % pieces)
            return 0

        lax.fori_loop(0, n * pieces, one, 0)

    def arrived(c, p, to, sent):
        relay_copy(c, p, to, sent).wait_recv()

        @pl.when((to >= 0) & (to < n))
        def _():
            relay_copy(c, p, to, sent).start()

        d = (b - c + n) % n

        @pl.when(d == r)
        def _():
            met_local(c, p).start()

        @pl.when(d != r)
        def _():
            met_copy(c, p, r, d).start()

    def relay_step(t, _):
        for i in range(fills):
            fill(t * fills + i)
        k = 1 + t // pieces
        p = t % pieces

        @pl.when(b - k >= 0)
        def _():
            arrived(b - k, p, b + 1, up_sent)

        @pl.when(b + k < n)
        def _():
            arrived(b + k, p, b - 1, down_sent)

        before = jnp.maximum(t - 1, 0)

        @pl.when((r != 0) & (t > 0) & (1 + before // pieces == wanted_steps))
        def _():
            forward_met(before % pieces)

        return 0

    lax.fori_loop(0, count, relay_step, 0)

    @pl.when((r != 0) & (wanted_steps == n - 1))
    def _():
        forward_met(pieces - 1)

    weight = jnp.float32(0.0)
    for other in range(n):
        for step in range(STEPS):
            weight = weight + jnp.where((offsets_ref[other] + step) % n == r, 1.0, 0.0)
    scale = weight / float(NG**3)

    wide = 4

    def across(i, _):
        k = wide * i
        both = jnp.concatenate(
            [field[pl.ds(k + w, NG, stride=plane), :] for w in range(wide)], axis=1
        )
        factor = jnp.concatenate(
            [table[pl.ds(pl.multiple_of((k + w) * NG, NG), NG), :] for w in range(wide)], axis=1
        )
        back = first_axis(first_axis(both, first_ref) * factor, first_ref)
        for w in range(wide):
            field[pl.ds(k + w, NG, stride=plane), :] = back[:, w * LANES : (w + 1) * LANES]
        return 0

    lax.fori_loop(0, plane // wide, across, 0)

    def backward(slot, p):
        here = quarter_piece(slot, p)
        potential = last_axis(middle_all(field[here, :]), main_ref, low_ref)
        return potential * (met[here, :] * scale)

    def pair_copy(i, p):
        return pltpu.make_async_remote_copy(
            src_ref=pair_out.at[i, at_piece(p)],
            dst_ref=pair_in.at[i, at_piece(p)],
            send_sem=pair_sent.at[i, p],
            recv_sem=pair_got.at[i, p],
            device_id={"blk": b, "rep": partner},
            device_id_type=MESH,
        )

    def cross_copy(i, p):
        return pltpu.make_async_remote_copy(
            src_ref=cross_out.at[i, at_piece(p)],
            dst_ref=cross_in.at[chips - i, at_piece(p)],
            send_sem=cross_sent.at[i, p],
            recv_sem=cross_got.at[chips - i, p],
            device_id={"blk": b, "rep": (chip + i) % chips * 2 + side},
            device_id_type=MESH,
        )

    def pair_quarter(i):
        def one(p, _):
            pair_out[i, at_piece(p), :] = backward((chip + i) % chips * 2 + 1 - side, p)
            pair_copy(i, p).start()
            return 0

        lax.fori_loop(0, pieces, one, 0)

    for i in range(1, chips):
        pair_quarter(i)

        def cross_step(p, _):
            mine = backward((chip + i) % chips * 2 + side, p)
            pair_copy(i, p).wait_recv()
            cross_out[i, at_piece(p), :] = mine + pair_in[i, at_piece(p), :]
            cross_copy(i, p).start()
            return 0

        lax.fori_loop(0, pieces, cross_step, 0)
    pair_quarter(0)

    def own_step(p, _):
        exchanged_ref[at_piece(p), :] = backward(r, p)
        return 0

    lax.fori_loop(0, pieces, own_step, 0)

    def total_step(p, sums):
        here = at_piece(p)
        pair_copy(0, p).wait_recv()
        total = exchanged_ref[here, :] + pair_in[0, here, :]
        for i in range(1, chips):
            cross_copy(chips - i, p).wait_recv()
            total = total + cross_in[i, here, :]
        exchanged_ref[here, :] = total

        def folded_sum(values):
            return jnp.sum((values * total).reshape(piece // 8, 8, LANES), axis=0)

        found = [folded_sum(psi_ref[quarter_piece(r, p), :])]
        for j in range(1, n):
            found.append(folded_sum(parts[(b + j) % n, here, :]))
        return tuple(s + f for s, f in zip(sums, found))

    zeros = jnp.zeros((8, LANES), jnp.float32)
    sums = lax.fori_loop(0, pieces, total_step, (zeros,) * n)
    sublane = lax.broadcasted_iota(jnp.int32, (8, LANES), 0)
    packed = jnp.zeros((8, LANES), jnp.float32)
    for j in range(n):
        line = jnp.sum(sums[j], axis=0, keepdims=True)
        packed = packed + jnp.where(sublane == (b + j) % n, line, 0.0)
    my_rows[...] = packed

    def rows_copy(to, source, j):
        return pltpu.make_async_remote_copy(
            src_ref=my_rows,
            dst_ref=all_rows.at[source],
            send_sem=rows_sent.at[j],
            recv_sem=rows_got.at[source],
            device_id=device(to),
            device_id_type=MESH,
        )

    for j in range(1, n * n):
        rows_copy((me + j) % (n * n), me, j).start()
    all_rows[me] = packed
    for j in range(1, n * n):
        source = (me + j) % (n * n)
        rows_copy(source, source, j).wait_recv()

    wanted = sublane == b
    place = lax.broadcasted_iota(jnp.int32, (1, n), 1)
    answer = jnp.zeros((1, n), jnp.float32)
    for c in range(n):
        whole = all_rows[c * n]
        for k in range(1, n):
            whole = whole + all_rows[c * n + k]
        value = jnp.sum(jnp.where(wanted, whole, 0.0)) / float(NG**3)
        answer = jnp.where(place == c, value, answer)
    margin_ref[...] = answer

    for j in range(1, n * n):
        rows_copy((me + j) % (n * n), me, j).wait_send()

    def sent_terms(p, _):
        for i in range(chips):
            pair_copy(i, p).wait_send()
        for i in range(1, chips):
            cross_copy(i, p).wait_send()

        @pl.when(b < n - 1)
        def _():
            own_copy(p, b + 1, up_sent).wait_send()

        @pl.when(b > 0)
        def _():
            own_copy(p, b - 1, down_sent).wait_send()

        return 0

    lax.fori_loop(0, pieces, sent_terms, 0)

    def left(c, p, to, sent):
        @pl.when((to >= 0) & (to < n))
        def _():
            relay_copy(c, p, to, sent).wait_send()

        d = (b - c + n) % n

        @pl.when(d != r)
        def _():
            met_copy(c, p, r, d).wait_send()

    def sent_step(t, _):
        k = 1 + t // pieces
        p = t % pieces

        @pl.when(b - k >= 0)
        def _():
            left(b - k, p, b + 1, up_sent)

        @pl.when(b + k < n)
        def _():
            left(b + k, p, b - 1, down_sent)

        return 0

    lax.fori_loop(0, count, sent_step, 0)


def local_distances(orbitals, offsets):
    n = lax.axis_size("blk")
    pieces = 4
    rows = orbitals.shape[1] // LANES
    quarter = rows // n
    chips = n // 2
    plane = NG * NG // LANES
    fills = pl.cdiv(plane, (n - 1) * pieces) * (n - 1) * pieces
    tables = cas_tables(NG)
    f32 = jnp.float32
    vmem = pl.BlockSpec(memory_space=pltpu.VMEM)
    dma = pltpu.SemaphoreType.DMA
    exchanged, margin = pl.pallas_call(
        functools.partial(exchange_kernel, n, pieces),
        out_shape=(
            jax.ShapeDtypeStruct((quarter, LANES), f32),
            jax.ShapeDtypeStruct((1, n), f32),
        ),
        in_specs=[pl.BlockSpec(memory_space=pltpu.SMEM)] + [vmem] * 5,
        out_specs=(vmem, vmem),
        scratch_shapes=[
            pltpu.VMEM((n, quarter, LANES), f32),
            pltpu.VMEM((rows, LANES), f32),
            pltpu.VMEM((rows, LANES), f32),
            pltpu.VMEM((fills * NG, LANES), f32),
            pltpu.VMEM((chips, quarter, LANES), f32),
            pltpu.VMEM((chips, quarter, LANES), f32),
            pltpu.VMEM((chips, quarter, LANES), f32),
            pltpu.VMEM((chips, quarter, LANES), f32),
            pltpu.VMEM((8, LANES), f32),
            pltpu.VMEM((n * n, 8, LANES), f32),
            dma((n, pieces)),
            dma((n, pieces)),
            dma((n, pieces)),
            dma((n, pieces)),
            dma((n, pieces)),
            dma((1 + pieces,)),
            dma((chips, pieces)),
            dma((chips, pieces)),
            dma((chips, pieces)),
            dma((chips, pieces)),
            dma((n * n,)),
            dma((n * n,)),
        ],
        compiler_params=pltpu.CompilerParams(
            collective_id=0, has_side_effects=True, vmem_limit_bytes=16 << 20
        ),
    )(offsets, orbitals.reshape(rows, LANES), *tables)
    return exchanged.reshape(1, quarter * LANES), margin


def solution(mesh):
    placed = (P(("groups", "blk"), None), P("groups"))
    one_each = mesh.shape["blk"] == mesh.shape["rep"] and mesh.shape["rep"] % 2 == 0
    local = local_distances if one_each else local_steps
    return jax.shard_map(
        local,
        mesh=mesh,
        in_specs=placed,
        out_specs=(P(("groups", "blk"), "rep"), P(("groups", "blk"), None)),
        check_vma=False,
    )
```

```python
import functools

import jax
import jax.numpy as jnp
import numpy as np
from jax import lax
from jax.experimental import pallas as pl
from jax.experimental.pallas import tpu as pltpu
from jax.sharding import PartitionSpec as P

NG = 64


precise_mode = lax.Precision.HIGHEST
solve_mode = lax.Precision.HIGH
STEPS = 3
screen_scale = 0.05


def passed_along(block, axis, distance):
    devices = range(lax.axis_size(axis))
    route = [((i - distance) % len(devices), i) for i in devices]
    return lax.ppermute(block, axis, route)


def cas_table(grid_points):
    grid_index = jnp.arange(grid_points, dtype=jnp.int32)
    product = grid_index[:, None] * grid_index[None, :] % grid_points
    phase_angle = 2.0 * jnp.pi / grid_points * product.astype(jnp.float32)
    return jnp.cos(phase_angle) + jnp.sin(phase_angle)


def screened_kernel(grid_points):
    grid_index = jnp.arange(grid_points, dtype=jnp.int32)
    folded = jnp.where(grid_index <= grid_points // 2, grid_index, grid_index - grid_points).astype(
        jnp.float32
    )
    squares = folded * folded
    k_squared = squares[:, None, None] + squares[None, :, None] + squares[None, None, :]
    safe_square = jnp.maximum(k_squared, 1.0)
    screened = (
        4.0
        * jnp.pi
        / (screen_scale * safe_square)
        * (1.0 - jnp.exp(-screen_scale * safe_square / (4.0 * jnp.pi)))
    )
    return jnp.where(k_squared > 0.5, screened, jnp.ones_like(screened))


def transform(values_field, cas_values, cas_paired):
    batch_size = values_field.shape[0]
    grid_points = values_field.shape[1]
    values_field = jnp.einsum(
        "kx,pxq->pkq",
        cas_values,
        values_field.reshape(batch_size, grid_points, grid_points * grid_points),
        precision=solve_mode,
    )
    values_field = jnp.einsum(
        "ky,ayz->akz",
        cas_values,
        values_field.reshape(batch_size * grid_points, grid_points, grid_points),
        precision=solve_mode,
    )
    values_field = jnp.dot(
        values_field.reshape(batch_size * grid_points * grid_points // 2, 2 * grid_points),
        cas_paired,
        precision=solve_mode,
    )
    return values_field.reshape(batch_size, grid_points, grid_points, grid_points)


def cycle_term(own_block, visiting, cas_values, cas_paired, kernel):
    grid_points = kernel.shape[0]
    block_rows = own_block.shape[0]
    density = (own_block[:, None, :] * visiting[None, :, :]).reshape(
        block_rows * block_rows, grid_points, grid_points, grid_points
    )
    spectrum = transform(density, cas_values, cas_paired) * kernel[None]
    potential = transform(spectrum, cas_values, cas_paired).reshape(
        block_rows, block_rows, grid_points**3
    ) / float(grid_points**3)
    return jnp.sum(potential * visiting[None, :, :], axis=1)


def position_block(orbital_block, amount):
    bit_count = (lax.axis_size("blk") - 1).bit_length()
    for bit_level in range(bit_count):
        moved_block = passed_along(orbital_block, "blk", 1 << bit_level)
        orbital_block = jnp.where(amount // (1 << bit_level) % 2 == 1, moved_block, orbital_block)
    return orbital_block


def finish(accumulator, orbitals):
    replica = lax.axis_index("rep")
    exchanged = lax.psum_scatter(accumulator, "rep", scatter_dimension=1, tiled=True)
    quarter_cells = exchanged.shape[1]
    quarter = lax.dynamic_slice_in_dim(orbitals, replica * quarter_cells, quarter_cells, 1)
    slab_orbitals, slab_exchanged = (
        lax.all_to_all(quarter, "blk", split_axis=1, concat_axis=0, tiled=True),
        lax.all_to_all(exchanged, "blk", split_axis=1, concat_axis=0, tiled=True),
    )
    partial_value = lax.dot_general(
        slab_orbitals, slab_exchanged, (((1,), (1,)), ((), ())), precision=precise_mode
    ) / float(NG**3)
    gram_rows = lax.psum_scatter(partial_value, "blk", scatter_dimension=0, tiled=True)
    margin = lax.psum(gram_rows, "rep")
    return (exchanged, margin)


def local_steps(orbitals, offsets):
    cas_values = cas_table(NG)
    cas_paired = jnp.kron(jnp.eye(2, dtype=jnp.float32), cas_values)
    kernel = screened_kernel(NG)
    cycle_size = lax.axis_size("blk")
    replica = lax.axis_index("rep")
    start_block = offsets[replica]
    first_visit = position_block(orbitals, (start_block + 1) % cycle_size)
    behind = passed_along(first_visit, "blk", -1)
    accumulator = cycle_term(orbitals, first_visit, cas_values, cas_paired, kernel)
    ahead_block = passed_along(first_visit, "blk", 1)
    accumulator = accumulator + cycle_term(orbitals, ahead_block, cas_values, cas_paired, kernel)
    accumulator = accumulator + cycle_term(orbitals, behind, cas_values, cas_paired, kernel)
    return finish(accumulator, orbitals)


MESH = pl.DeviceIdType.MESH
LANES = 128


def two_halves(table):
    high = table.astype(jnp.bfloat16)
    low = (table - high.astype(np.float64)).astype(jnp.bfloat16)
    return high, low


def cas_tables(grid_points):
    index = np.arange(grid_points)
    angle = 2.0 * np.pi / grid_points * (np.outer(index, index) % grid_points)
    cas = np.cos(angle) + np.sin(angle)
    high, low = two_halves(np.kron(np.eye(2), cas))
    last_main = np.concatenate([high, high], axis=0)
    blocks = [cas[k::2, y::2] for k in range(2) for y in range(2)]
    y_high, y_low = two_halves(np.concatenate(blocks, axis=0))
    middle = np.concatenate([y_high, y_high, y_low], axis=1)
    x_high, x_low = two_halves(cas)
    first = np.concatenate([x_high, x_high, x_low], axis=1)
    return [jnp.asarray(t) for t in (last_main, low, middle, first)]


def split(values):
    high = values.astype(jnp.bfloat16)
    return high, (values - high.astype(jnp.float32)).astype(jnp.bfloat16)


def dot(a, b):
    return jnp.dot(a, b, preferred_element_type=jnp.float32)


def last_axis(values, main_ref, low_ref):
    high, low = split(values)
    return dot(jnp.concatenate([high, low], axis=1), main_ref[...]) + dot(high, low_ref[...])


def middle_axis(pair, middle_ref):
    half = pair.shape[0]
    high, low = split(pair)
    terms = dot(middle_ref[...], jnp.concatenate([high, low, high], axis=0))
    lane = lax.broadcasted_iota(jnp.int32, (half, pair.shape[1]), 1) % LANES
    first = lane < LANES // 2
    t = [terms[i * half : (i + 1) * half] for i in range(4)]
    straight = jnp.where(first, t[0], t[3])
    crossed = jnp.where(first, t[2], t[1])
    return [
        straight[:, at : at + LANES] + pltpu.roll(crossed[:, at : at + LANES], LANES // 2, 1)
        for at in (0, LANES)
    ]


def first_axis(values, first_ref):
    high, low = split(values)
    return dot(first_ref[...], jnp.concatenate([high, low, high], axis=0))


def exchange_kernel(
    n,
    pieces,
    offsets_ref,
    psi_ref,
    main_ref,
    low_ref,
    middle_ref,
    first_ref,
    exchanged_ref,
    margin_ref,
    parts,
    met,
    field,
    table,
    pair_out,
    pair_in,
    cross_out,
    cross_in,
    my_rows,
    all_rows,
    up_sent,
    down_sent,
    part_got,
    met_sent,
    met_got,
    local_sem,
    pair_sent,
    pair_got,
    cross_sent,
    cross_got,
    rows_sent,
    rows_got,
):
    b = lax.axis_index("blk")
    r = lax.axis_index("rep")
    rows = psi_ref.shape[0]
    quarter = rows // n
    piece = quarter // pieces
    plane = NG * NG // LANES
    batch = piece // plane
    me = b * n + r
    chips = n // 2
    chip = r // 2
    side = r % 2
    partner = r + 1 - 2 * side

    def device(at):
        return {"blk": at // n, "rep": at % n}

    barrier = pltpu.get_barrier_semaphore()
    for j in range(1, n * n):
        pl.semaphore_signal(
            barrier, inc=1, device_id=device((me + j) % (n * n)), device_id_type=MESH
        )
    pl.semaphore_wait(barrier, n * n - 1)

    def at_piece(p):
        return pl.ds(pl.multiple_of(p * piece, 8), piece)

    def quarter_piece(slot, p):
        return pl.ds(pl.multiple_of(slot * quarter + p * piece, 8), piece)

    def part_copy(source, c, p, to, sent):
        return pltpu.make_async_remote_copy(
            src_ref=source,
            dst_ref=parts.at[c, at_piece(p)],
            send_sem=sent.at[c, p],
            recv_sem=part_got.at[c, p],
            device_id={"blk": to, "rep": r},
            device_id_type=MESH,
        )

    def own_copy(p, to, sent):
        return part_copy(psi_ref.at[quarter_piece(r, p)], b, p, to, sent)

    def relay_copy(c, p, to, sent):
        return part_copy(parts.at[c, at_piece(p)], c, p, to, sent)

    @pl.when(b < n - 1)
    def _():
        for p in range(pieces):
            own_copy(p, b + 1, up_sent).start()

    @pl.when(b > 0)
    def _():
        for p in range(pieces):
            own_copy(p, b - 1, down_sent).start()

    whole_copy = pltpu.make_async_copy(psi_ref, met, local_sem.at[0])

    @pl.when(r == 0)
    def _():
        whole_copy.start()

    def folded(index):
        return jnp.where(index <= NG // 2, index, index - NG).astype(jnp.float32)

    lane = lax.broadcasted_iota(jnp.int32, (NG, LANES), 1)
    kx = folded(lax.broadcasted_iota(jnp.int32, (NG, LANES), 0))
    kz = folded(lane % NG)
    base = kx * kx + kz * kz

    def fill(k):
        ky = folded(2 * k + lane // NG)
        k_squared = base + ky * ky
        safe = jnp.maximum(k_squared, 1.0)
        scaled = screen_scale * safe / (4.0 * jnp.pi)
        screened = (1.0 - jnp.exp(-scaled)) / scaled
        start = pl.multiple_of(k * NG, NG)
        table[pl.ds(start, NG), :] = jnp.where(k_squared > 0.5, screened, 1.0)

    def met_copy(c, p, slot, d):
        return pltpu.make_async_remote_copy(
            src_ref=parts.at[c, at_piece(p)],
            dst_ref=met.at[quarter_piece(slot, p)],
            send_sem=met_sent.at[d, p],
            recv_sem=met_got.at[slot, p],
            device_id={"blk": b, "rep": d},
            device_id_type=MESH,
        )

    def met_local(c, p):
        return pltpu.make_async_copy(
            parts.at[c, at_piece(p)], met.at[quarter_piece(r, p)], local_sem.at[1 + p]
        )

    def planes_of(values):
        return [values[i * plane : (i + 1) * plane] for i in range(batch)]

    def middle_all(values):
        whole = planes_of(values)
        turned = []
        for i in range(0, batch, 2):
            pair = jnp.concatenate([whole[i], whole[i + 1]], axis=1)
            turned += middle_axis(pair, middle_ref)
        return jnp.concatenate(turned, axis=0)

    def forward(slot, p):
        here = quarter_piece(slot, p)
        density = psi_ref[here, :] * met[here, :]
        field[here, :] = middle_all(last_axis(density, main_ref, low_ref))

    def forward_met(p):
        met_local(b, p).wait()
        forward(r, p)

        def one(j, _):
            slot = (r + j) % n
            met_copy(b, p, slot, slot).wait_recv()
            forward(slot, p)
            return 0

        lax.fori_loop(1, n, one, 0)

    count = (n - 1) * pieces
    fills = pl.cdiv(plane, count)
    wanted_block = (b - r + n) % n
    wanted_steps = jnp.maximum(wanted_block - b, b - wanted_block)

    @pl.when(r == 0)
    def _():
        whole_copy.wait()

        def one(t, _):
            forward(t // pieces, t % pieces)
            return 0

        lax.fori_loop(0, n * pieces, one, 0)

    def arrived(c, p, to, sent):
        relay_copy(c, p, to, sent).wait_recv()

        @pl.when((to >= 0) & (to < n))
        def _():
            relay_copy(c, p, to, sent).start()

        d = (b - c + n) % n

        @pl.when(d == r)
        def _():
            met_local(c, p).start()

        @pl.when(d != r)
        def _():
            met_copy(c, p, r, d).start()

    def relay_step(t, _):
        for i in range(fills):
            fill(t * fills + i)
        k = 1 + t // pieces
        p = t % pieces

        @pl.when(b - k >= 0)
        def _():
            arrived(b - k, p, b + 1, up_sent)

        @pl.when(b + k < n)
        def _():
            arrived(b + k, p, b - 1, down_sent)

        before = jnp.maximum(t - 1, 0)

        @pl.when((r != 0) & (t > 0) & (1 + before // pieces == wanted_steps))
        def _():
            forward_met(before % pieces)

        return 0

    lax.fori_loop(0, count, relay_step, 0)

    @pl.when((r != 0) & (wanted_steps == n - 1))
    def _():
        forward_met(pieces - 1)

    weight = jnp.float32(0.0)
    for other in range(n):
        for step in range(STEPS):
            weight = weight + jnp.where((offsets_ref[other] + step) % n == r, 1.0, 0.0)
    scale = weight / float(NG**3)

    wide = 16

    def across(i, _):
        k = wide * i
        both = jnp.concatenate(
            [field[pl.ds(k + w, NG, stride=plane), :] for w in range(wide)], axis=1
        )
        factor = jnp.concatenate(
            [table[pl.ds(pl.multiple_of((k + w) * NG, NG), NG), :] for w in range(wide)], axis=1
        )
        back = first_axis(first_axis(both, first_ref) * factor, first_ref)
        for w in range(wide):
            field[pl.ds(k + w, NG, stride=plane), :] = back[:, w * LANES : (w + 1) * LANES]
        return 0

    lax.fori_loop(0, plane // wide, across, 0)

    def backward(slot, p):
        here = quarter_piece(slot, p)
        potential = last_axis(middle_all(field[here, :]), main_ref, low_ref)
        return potential * (met[here, :] * scale)

    def pair_copy(i, p):
        return pltpu.make_async_remote_copy(
            src_ref=pair_out.at[i, at_piece(p)],
            dst_ref=pair_in.at[i, at_piece(p)],
            send_sem=pair_sent.at[i, p],
            recv_sem=pair_got.at[i, p],
            device_id={"blk": b, "rep": partner},
            device_id_type=MESH,
        )

    def cross_copy(i, p):
        return pltpu.make_async_remote_copy(
            src_ref=cross_out.at[i, at_piece(p)],
            dst_ref=cross_in.at[chips - i, at_piece(p)],
            send_sem=cross_sent.at[i, p],
            recv_sem=cross_got.at[chips - i, p],
            device_id={"blk": b, "rep": (chip + i) % chips * 2 + side},
            device_id_type=MESH,
        )

    def pair_quarter(i):
        def one(p, _):
            pair_out[i, at_piece(p), :] = backward((chip + i) % chips * 2 + 1 - side, p)
            pair_copy(i, p).start()
            return 0

        lax.fori_loop(0, pieces, one, 0)

    for i in range(1, chips):
        pair_quarter(i)

        def cross_step(p, _):
            mine = backward((chip + i) % chips * 2 + side, p)
            pair_copy(i, p).wait_recv()
            cross_out[i, at_piece(p), :] = mine + pair_in[i, at_piece(p), :]
            cross_copy(i, p).start()
            return 0

        lax.fori_loop(0, pieces, cross_step, 0)
    pair_quarter(0)

    def own_step(p, _):
        exchanged_ref[at_piece(p), :] = backward(r, p)
        return 0

    lax.fori_loop(0, pieces, own_step, 0)

    def total_step(p, sums):
        here = at_piece(p)
        pair_copy(0, p).wait_recv()
        total = exchanged_ref[here, :] + pair_in[0, here, :]
        for i in range(1, chips):
            cross_copy(chips - i, p).wait_recv()
            total = total + cross_in[i, here, :]
        exchanged_ref[here, :] = total

        def folded_sum(values):
            return jnp.sum((values * total).reshape(piece // 8, 8, LANES), axis=0)

        found = [folded_sum(psi_ref[quarter_piece(r, p), :])]
        for j in range(1, n):
            found.append(folded_sum(parts[(b + j) % n, here, :]))
        return tuple(s + f for s, f in zip(sums, found))

    zeros = jnp.zeros((8, LANES), jnp.float32)
    sums = lax.fori_loop(0, pieces, total_step, (zeros,) * n)
    sublane = lax.broadcasted_iota(jnp.int32, (8, LANES), 0)
    packed = jnp.zeros((8, LANES), jnp.float32)
    for j in range(n):
        line = jnp.sum(sums[j], axis=0, keepdims=True)
        packed = packed + jnp.where(sublane == (b + j) % n, line, 0.0)
    my_rows[...] = packed

    def rows_copy(to, source, j):
        return pltpu.make_async_remote_copy(
            src_ref=my_rows,
            dst_ref=all_rows.at[source],
            send_sem=rows_sent.at[j],
            recv_sem=rows_got.at[source],
            device_id=device(to),
            device_id_type=MESH,
        )

    for j in range(1, n * n):
        rows_copy((me + j) % (n * n), me, j).start()
    all_rows[me] = packed
    for j in range(1, n * n):
        source = (me + j) % (n * n)
        rows_copy(source, source, j).wait_recv()

    wanted = sublane == b
    place = lax.broadcasted_iota(jnp.int32, (1, n), 1)
    answer = jnp.zeros((1, n), jnp.float32)
    for c in range(n):
        whole = all_rows[c * n]
        for k in range(1, n):
            whole = whole + all_rows[c * n + k]
        value = jnp.sum(jnp.where(wanted, whole, 0.0)) / float(NG**3)
        answer = jnp.where(place == c, value, answer)
    margin_ref[...] = answer

    for j in range(1, n * n):
        rows_copy((me + j) % (n * n), me, j).wait_send()

    def sent_terms(p, _):
        for i in range(chips):
            pair_copy(i, p).wait_send()
        for i in range(1, chips):
            cross_copy(i, p).wait_send()

        @pl.when(b < n - 1)
        def _():
            own_copy(p, b + 1, up_sent).wait_send()

        @pl.when(b > 0)
        def _():
            own_copy(p, b - 1, down_sent).wait_send()

        return 0

    lax.fori_loop(0, pieces, sent_terms, 0)

    def left(c, p, to, sent):
        @pl.when((to >= 0) & (to < n))
        def _():
            relay_copy(c, p, to, sent).wait_send()

        d = (b - c + n) % n

        @pl.when(d != r)
        def _():
            met_copy(c, p, r, d).wait_send()

    def sent_step(t, _):
        k = 1 + t // pieces
        p = t % pieces

        @pl.when(b - k >= 0)
        def _():
            left(b - k, p, b + 1, up_sent)

        @pl.when(b + k < n)
        def _():
            left(b + k, p, b - 1, down_sent)

        return 0

    lax.fori_loop(0, count, sent_step, 0)


def local_distances(orbitals, offsets):
    n = lax.axis_size("blk")
    pieces = 2
    rows = orbitals.shape[1] // LANES
    quarter = rows // n
    chips = n // 2
    plane = NG * NG // LANES
    fills = pl.cdiv(plane, (n - 1) * pieces) * (n - 1) * pieces
    tables = cas_tables(NG)
    f32 = jnp.float32
    vmem = pl.BlockSpec(memory_space=pltpu.VMEM)
    dma = pltpu.SemaphoreType.DMA
    exchanged, margin = pl.pallas_call(
        functools.partial(exchange_kernel, n, pieces),
        out_shape=(
            jax.ShapeDtypeStruct((quarter, LANES), f32),
            jax.ShapeDtypeStruct((1, n), f32),
        ),
        in_specs=[pl.BlockSpec(memory_space=pltpu.SMEM)] + [vmem] * 5,
        out_specs=(vmem, vmem),
        scratch_shapes=[
            pltpu.VMEM((n, quarter, LANES), f32),
            pltpu.VMEM((rows, LANES), f32),
            pltpu.VMEM((rows, LANES), f32),
            pltpu.VMEM((fills * NG, LANES), f32),
            pltpu.VMEM((chips, quarter, LANES), f32),
            pltpu.VMEM((chips, quarter, LANES), f32),
            pltpu.VMEM((chips, quarter, LANES), f32),
            pltpu.VMEM((chips, quarter, LANES), f32),
            pltpu.VMEM((8, LANES), f32),
            pltpu.VMEM((n * n, 8, LANES), f32),
            dma((n, pieces)),
            dma((n, pieces)),
            dma((n, pieces)),
            dma((n, pieces)),
            dma((n, pieces)),
            dma((1 + pieces,)),
            dma((chips, pieces)),
            dma((chips, pieces)),
            dma((chips, pieces)),
            dma((chips, pieces)),
            dma((n * n,)),
            dma((n * n,)),
        ],
        compiler_params=pltpu.CompilerParams(
            collective_id=0, has_side_effects=True, vmem_limit_bytes=16 << 20
        ),
    )(offsets, orbitals.reshape(rows, LANES), *tables)
    return exchanged.reshape(1, quarter * LANES), margin


def solution(mesh):
    placed = (P(("groups", "blk"), None), P("groups"))
    one_each = mesh.shape["blk"] == mesh.shape["rep"] and mesh.shape["rep"] % 2 == 0
    local = local_distances if one_each else local_steps
    return jax.shard_map(
        local,
        mesh=mesh,
        in_specs=placed,
        out_specs=(P(("groups", "blk"), "rep"), P(("groups", "blk"), None)),
        check_vma=False,
    )
```

```python
import functools

import jax
import jax.numpy as jnp
import numpy as np
from jax import lax
from jax.experimental import pallas as pl
from jax.experimental.pallas import tpu as pltpu
from jax.sharding import PartitionSpec as P

NG = 64


precise_mode = lax.Precision.HIGHEST
solve_mode = lax.Precision.HIGH
STEPS = 3
screen_scale = 0.05


def passed_along(block, axis, distance):
    devices = range(lax.axis_size(axis))
    route = [((i - distance) % len(devices), i) for i in devices]
    return lax.ppermute(block, axis, route)


def cas_table(grid_points):
    grid_index = jnp.arange(grid_points, dtype=jnp.int32)
    product = grid_index[:, None] * grid_index[None, :] % grid_points
    phase_angle = 2.0 * jnp.pi / grid_points * product.astype(jnp.float32)
    return jnp.cos(phase_angle) + jnp.sin(phase_angle)


def screened_kernel(grid_points):
    grid_index = jnp.arange(grid_points, dtype=jnp.int32)
    folded = jnp.where(grid_index <= grid_points // 2, grid_index, grid_index - grid_points).astype(
        jnp.float32
    )
    squares = folded * folded
    k_squared = squares[:, None, None] + squares[None, :, None] + squares[None, None, :]
    safe_square = jnp.maximum(k_squared, 1.0)
    screened = (
        4.0
        * jnp.pi
        / (screen_scale * safe_square)
        * (1.0 - jnp.exp(-screen_scale * safe_square / (4.0 * jnp.pi)))
    )
    return jnp.where(k_squared > 0.5, screened, jnp.ones_like(screened))


def transform(values_field, cas_values, cas_paired):
    batch_size = values_field.shape[0]
    grid_points = values_field.shape[1]
    values_field = jnp.einsum(
        "kx,pxq->pkq",
        cas_values,
        values_field.reshape(batch_size, grid_points, grid_points * grid_points),
        precision=solve_mode,
    )
    values_field = jnp.einsum(
        "ky,ayz->akz",
        cas_values,
        values_field.reshape(batch_size * grid_points, grid_points, grid_points),
        precision=solve_mode,
    )
    values_field = jnp.dot(
        values_field.reshape(batch_size * grid_points * grid_points // 2, 2 * grid_points),
        cas_paired,
        precision=solve_mode,
    )
    return values_field.reshape(batch_size, grid_points, grid_points, grid_points)


def cycle_term(own_block, visiting, cas_values, cas_paired, kernel):
    grid_points = kernel.shape[0]
    block_rows = own_block.shape[0]
    density = (own_block[:, None, :] * visiting[None, :, :]).reshape(
        block_rows * block_rows, grid_points, grid_points, grid_points
    )
    spectrum = transform(density, cas_values, cas_paired) * kernel[None]
    potential = transform(spectrum, cas_values, cas_paired).reshape(
        block_rows, block_rows, grid_points**3
    ) / float(grid_points**3)
    return jnp.sum(potential * visiting[None, :, :], axis=1)


def position_block(orbital_block, amount):
    bit_count = (lax.axis_size("blk") - 1).bit_length()
    for bit_level in range(bit_count):
        moved_block = passed_along(orbital_block, "blk", 1 << bit_level)
        orbital_block = jnp.where(amount // (1 << bit_level) % 2 == 1, moved_block, orbital_block)
    return orbital_block


def finish(accumulator, orbitals):
    replica = lax.axis_index("rep")
    exchanged = lax.psum_scatter(accumulator, "rep", scatter_dimension=1, tiled=True)
    quarter_cells = exchanged.shape[1]
    quarter = lax.dynamic_slice_in_dim(orbitals, replica * quarter_cells, quarter_cells, 1)
    slab_orbitals, slab_exchanged = (
        lax.all_to_all(quarter, "blk", split_axis=1, concat_axis=0, tiled=True),
        lax.all_to_all(exchanged, "blk", split_axis=1, concat_axis=0, tiled=True),
    )
    partial_value = lax.dot_general(
        slab_orbitals, slab_exchanged, (((1,), (1,)), ((), ())), precision=precise_mode
    ) / float(NG**3)
    gram_rows = lax.psum_scatter(partial_value, "blk", scatter_dimension=0, tiled=True)
    margin = lax.psum(gram_rows, "rep")
    return (exchanged, margin)


def local_steps(orbitals, offsets):
    cas_values = cas_table(NG)
    cas_paired = jnp.kron(jnp.eye(2, dtype=jnp.float32), cas_values)
    kernel = screened_kernel(NG)
    cycle_size = lax.axis_size("blk")
    replica = lax.axis_index("rep")
    start_block = offsets[replica]
    first_visit = position_block(orbitals, (start_block + 1) % cycle_size)
    behind = passed_along(first_visit, "blk", -1)
    accumulator = cycle_term(orbitals, first_visit, cas_values, cas_paired, kernel)
    ahead_block = passed_along(first_visit, "blk", 1)
    accumulator = accumulator + cycle_term(orbitals, ahead_block, cas_values, cas_paired, kernel)
    accumulator = accumulator + cycle_term(orbitals, behind, cas_values, cas_paired, kernel)
    return finish(accumulator, orbitals)


MESH = pl.DeviceIdType.MESH
LANES = 128


def two_halves(table):
    high = table.astype(jnp.bfloat16)
    low = (table - high.astype(np.float64)).astype(jnp.bfloat16)
    return high, low


def cas_tables(grid_points):
    index = np.arange(grid_points)
    angle = 2.0 * np.pi / grid_points * (np.outer(index, index) % grid_points)
    cas = np.cos(angle) + np.sin(angle)
    high, low = two_halves(np.kron(np.eye(2), cas))
    last_main = np.concatenate([high, high], axis=0)
    blocks = [cas[k::2, y::2] for k in range(2) for y in range(2)]
    y_high, y_low = two_halves(np.concatenate(blocks, axis=0))
    middle = np.concatenate([y_high, y_high, y_low], axis=1)
    x_high, x_low = two_halves(cas)
    first = np.concatenate([x_high, x_high, x_low], axis=1)
    return [jnp.asarray(t) for t in (last_main, low, middle, first)]


def split(values):
    high = values.astype(jnp.bfloat16)
    return high, (values - high.astype(jnp.float32)).astype(jnp.bfloat16)


def dot(a, b):
    return jnp.dot(a, b, preferred_element_type=jnp.float32)


def last_axis(values, main_ref, low_ref):
    high, low = split(values)
    return dot(jnp.concatenate([high, low], axis=1), main_ref[...]) + dot(high, low_ref[...])


def middle_axis(pair, middle_ref):
    half = pair.shape[0]
    high, low = split(pair)
    terms = dot(middle_ref[...], jnp.concatenate([high, low, high], axis=0))
    lane = lax.broadcasted_iota(jnp.int32, (half, pair.shape[1]), 1) % LANES
    first = lane < LANES // 2
    t = [terms[i * half : (i + 1) * half] for i in range(4)]
    straight = jnp.where(first, t[0], t[3])
    crossed = jnp.where(first, t[2], t[1])
    return [
        straight[:, at : at + LANES] + pltpu.roll(crossed[:, at : at + LANES], LANES // 2, 1)
        for at in (0, LANES)
    ]


def first_axis(values, first_ref):
    high, low = split(values)
    return dot(first_ref[...], jnp.concatenate([high, low, high], axis=0))


def exchange_kernel(
    n,
    pieces,
    offsets_ref,
    psi_ref,
    main_ref,
    low_ref,
    middle_ref,
    first_ref,
    exchanged_ref,
    margin_ref,
    parts,
    met,
    field,
    table,
    pair_out,
    pair_in,
    cross_out,
    cross_in,
    my_rows,
    all_rows,
    up_sent,
    down_sent,
    part_got,
    met_sent,
    met_got,
    local_sem,
    pair_sent,
    pair_got,
    cross_sent,
    cross_got,
    rows_sent,
    rows_got,
):
    b = lax.axis_index("blk")
    r = lax.axis_index("rep")
    rows = psi_ref.shape[0]
    quarter = rows // n
    piece = quarter // pieces
    plane = NG * NG // LANES
    batch = piece // plane
    me = b * n + r
    chips = n // 2
    chip = r // 2
    side = r % 2
    partner = r + 1 - 2 * side

    def device(at):
        return {"blk": at // n, "rep": at % n}

    barrier = pltpu.get_barrier_semaphore()
    for j in range(1, n * n):
        pl.semaphore_signal(
            barrier, inc=1, device_id=device((me + j) % (n * n)), device_id_type=MESH
        )
    pl.semaphore_wait(barrier, n * n - 1)

    def at_piece(p):
        return pl.ds(pl.multiple_of(p * piece, 8), piece)

    def quarter_piece(slot, p):
        return pl.ds(pl.multiple_of(slot * quarter + p * piece, 8), piece)

    def part_copy(source, c, p, to, sent):
        return pltpu.make_async_remote_copy(
            src_ref=source,
            dst_ref=parts.at[c, at_piece(p)],
            send_sem=sent.at[c, p],
            recv_sem=part_got.at[c, p],
            device_id={"blk": to, "rep": r},
            device_id_type=MESH,
        )

    def own_copy(p, to, sent):
        return part_copy(psi_ref.at[quarter_piece(r, p)], b, p, to, sent)

    def relay_copy(c, p, to, sent):
        return part_copy(parts.at[c, at_piece(p)], c, p, to, sent)

    @pl.when(b < n - 1)
    def _():
        for p in range(pieces):
            own_copy(p, b + 1, up_sent).start()

    @pl.when(b > 0)
    def _():
        for p in range(pieces):
            own_copy(p, b - 1, down_sent).start()

    whole_copy = pltpu.make_async_copy(psi_ref, met, local_sem.at[0])

    @pl.when(r == 0)
    def _():
        whole_copy.start()

    def folded(index):
        return jnp.where(index <= NG // 2, index, index - NG).astype(jnp.float32)

    lane = lax.broadcasted_iota(jnp.int32, (NG, LANES), 1)
    kx = folded(lax.broadcasted_iota(jnp.int32, (NG, LANES), 0))
    kz = folded(lane % NG)
    base = kx * kx + kz * kz

    def fill(k):
        ky = folded(2 * k + lane // NG)
        k_squared = base + ky * ky
        safe = jnp.maximum(k_squared, 1.0)
        scaled = screen_scale * safe / (4.0 * jnp.pi)
        screened = (1.0 - jnp.exp(-scaled)) / scaled
        start = pl.multiple_of(k * NG, NG)
        table[pl.ds(start, NG), :] = jnp.where(k_squared > 0.5, screened, 1.0)

    def met_copy(c, p, slot, d):
        return pltpu.make_async_remote_copy(
            src_ref=parts.at[c, at_piece(p)],
            dst_ref=met.at[quarter_piece(slot, p)],
            send_sem=met_sent.at[d, p],
            recv_sem=met_got.at[slot, p],
            device_id={"blk": b, "rep": d},
            device_id_type=MESH,
        )

    def met_local(c, p):
        return pltpu.make_async_copy(
            parts.at[c, at_piece(p)], met.at[quarter_piece(r, p)], local_sem.at[1 + p]
        )

    def planes_of(values):
        return [values[i * plane : (i + 1) * plane] for i in range(batch)]

    def middle_all(values):
        whole = planes_of(values)
        turned = []
        for i in range(0, batch, 2):
            pair = jnp.concatenate([whole[i], whole[i + 1]], axis=1)
            turned += middle_axis(pair, middle_ref)
        return jnp.concatenate(turned, axis=0)

    def forward(slot, p):
        here = quarter_piece(slot, p)
        density = psi_ref[here, :] * met[here, :]
        field[here, :] = middle_all(last_axis(density, main_ref, low_ref))

    def forward_met(p):
        met_local(b, p).wait()
        forward(r, p)

        def one(j, _):
            slot = (r + j) % n
            met_copy(b, p, slot, slot).wait_recv()
            forward(slot, p)
            return 0

        lax.fori_loop(1, n, one, 0)

    count = (n - 1) * pieces
    fills = pl.cdiv(plane, count)
    own_batches = pl.cdiv(n * pieces, count)
    wanted_block = (b - r + n) % n
    wanted_steps = jnp.maximum(wanted_block - b, b - wanted_block)

    @pl.when(r == 0)
    def _():
        whole_copy.wait()

    def arrived(c, p, to, sent):
        relay_copy(c, p, to, sent).wait_recv()

        @pl.when((to >= 0) & (to < n))
        def _():
            relay_copy(c, p, to, sent).start()

        d = (b - c + n) % n

        @pl.when(d == r)
        def _():
            met_local(c, p).start()

        @pl.when(d != r)
        def _():
            met_copy(c, p, r, d).start()

    def relay_step(t, _):
        for i in range(fills):
            fill(t * fills + i)
        k = 1 + t // pieces
        p = t % pieces

        @pl.when(b - k >= 0)
        def _():
            arrived(b - k, p, b + 1, up_sent)

        @pl.when(b + k < n)
        def _():
            arrived(b + k, p, b - 1, down_sent)

        def own_forward(i, _):
            at = t * own_batches + i

            @pl.when(at < n * pieces)
            def _():
                forward(at // pieces, at % pieces)

            return 0

        @pl.when(r == 0)
        def _():
            lax.fori_loop(0, own_batches, own_forward, 0)

        before = jnp.maximum(t - 1, 0)

        @pl.when((r != 0) & (t > 0) & (1 + before // pieces == wanted_steps))
        def _():
            forward_met(before % pieces)

        return 0

    lax.fori_loop(0, count, relay_step, 0)

    @pl.when((r != 0) & (wanted_steps == n - 1))
    def _():
        forward_met(pieces - 1)

    weight = jnp.float32(0.0)
    for other in range(n):
        for step in range(STEPS):
            weight = weight + jnp.where((offsets_ref[other] + step) % n == r, 1.0, 0.0)
    scale = weight / float(NG**3)

    wide = 16

    def across(i, _):
        k = wide * i
        both = jnp.concatenate(
            [field[pl.ds(k + w, NG, stride=plane), :] for w in range(wide)], axis=1
        )
        factor = jnp.concatenate(
            [table[pl.ds(pl.multiple_of((k + w) * NG, NG), NG), :] for w in range(wide)], axis=1
        )
        back = first_axis(first_axis(both, first_ref) * factor, first_ref)
        for w in range(wide):
            field[pl.ds(k + w, NG, stride=plane), :] = back[:, w * LANES : (w + 1) * LANES]
        return 0

    lax.fori_loop(0, plane // wide, across, 0)

    def backward(slot, p):
        here = quarter_piece(slot, p)
        potential = last_axis(middle_all(field[here, :]), main_ref, low_ref)
        return potential * (met[here, :] * scale)

    def pair_copy(i, p):
        return pltpu.make_async_remote_copy(
            src_ref=pair_out.at[i, at_piece(p)],
            dst_ref=pair_in.at[i, at_piece(p)],
            send_sem=pair_sent.at[i, p],
            recv_sem=pair_got.at[i, p],
            device_id={"blk": b, "rep": partner},
            device_id_type=MESH,
        )

    def cross_copy(i, p):
        return pltpu.make_async_remote_copy(
            src_ref=cross_out.at[i, at_piece(p)],
            dst_ref=cross_in.at[chips - i, at_piece(p)],
            send_sem=cross_sent.at[i, p],
            recv_sem=cross_got.at[chips - i, p],
            device_id={"blk": b, "rep": (chip + i) % chips * 2 + side},
            device_id_type=MESH,
        )

    def pair_quarter(i):
        def one(p, _):
            pair_out[i, at_piece(p), :] = backward((chip + i) % chips * 2 + 1 - side, p)
            pair_copy(i, p).start()
            return 0

        lax.fori_loop(0, pieces, one, 0)

    for i in range(1, chips):
        pair_quarter(i)

        def cross_step(p, _):
            mine = backward((chip + i) % chips * 2 + side, p)
            pair_copy(i, p).wait_recv()
            cross_out[i, at_piece(p), :] = mine + pair_in[i, at_piece(p), :]
            cross_copy(i, p).start()
            return 0

        lax.fori_loop(0, pieces, cross_step, 0)
    pair_quarter(0)

    def own_step(p, _):
        exchanged_ref[at_piece(p), :] = backward(r, p)
        return 0

    lax.fori_loop(0, pieces, own_step, 0)

    def total_step(p, sums):
        here = at_piece(p)
        pair_copy(0, p).wait_recv()
        total = exchanged_ref[here, :] + pair_in[0, here, :]
        for i in range(1, chips):
            cross_copy(chips - i, p).wait_recv()
            total = total + cross_in[i, here, :]
        exchanged_ref[here, :] = total

        def folded_sum(values):
            return jnp.sum((values * total).reshape(piece // 8, 8, LANES), axis=0)

        found = [folded_sum(psi_ref[quarter_piece(r, p), :])]
        for j in range(1, n):
            found.append(folded_sum(parts[(b + j) % n, here, :]))
        return tuple(s + f for s, f in zip(sums, found))

    zeros = jnp.zeros((8, LANES), jnp.float32)
    sums = lax.fori_loop(0, pieces, total_step, (zeros,) * n)
    sublane = lax.broadcasted_iota(jnp.int32, (8, LANES), 0)
    packed = jnp.zeros((8, LANES), jnp.float32)
    for j in range(n):
        line = jnp.sum(sums[j], axis=0, keepdims=True)
        packed = packed + jnp.where(sublane == (b + j) % n, line, 0.0)
    my_rows[...] = packed

    def rows_copy(to, source, j):
        return pltpu.make_async_remote_copy(
            src_ref=my_rows,
            dst_ref=all_rows.at[source],
            send_sem=rows_sent.at[j],
            recv_sem=rows_got.at[source],
            device_id=device(to),
            device_id_type=MESH,
        )

    for j in range(1, n * n):
        rows_copy((me + j) % (n * n), me, j).start()
    all_rows[me] = packed
    for j in range(1, n * n):
        source = (me + j) % (n * n)
        rows_copy(source, source, j).wait_recv()

    wanted = sublane == b
    place = lax.broadcasted_iota(jnp.int32, (1, n), 1)
    answer = jnp.zeros((1, n), jnp.float32)
    for c in range(n):
        whole = all_rows[c * n]
        for k in range(1, n):
            whole = whole + all_rows[c * n + k]
        value = jnp.sum(jnp.where(wanted, whole, 0.0)) / float(NG**3)
        answer = jnp.where(place == c, value, answer)
    margin_ref[...] = answer

    for j in range(1, n * n):
        rows_copy((me + j) % (n * n), me, j).wait_send()

    def sent_terms(p, _):
        for i in range(chips):
            pair_copy(i, p).wait_send()
        for i in range(1, chips):
            cross_copy(i, p).wait_send()

        @pl.when(b < n - 1)
        def _():
            own_copy(p, b + 1, up_sent).wait_send()

        @pl.when(b > 0)
        def _():
            own_copy(p, b - 1, down_sent).wait_send()

        return 0

    lax.fori_loop(0, pieces, sent_terms, 0)

    def left(c, p, to, sent):
        @pl.when((to >= 0) & (to < n))
        def _():
            relay_copy(c, p, to, sent).wait_send()

        d = (b - c + n) % n

        @pl.when(d != r)
        def _():
            met_copy(c, p, r, d).wait_send()

    def sent_step(t, _):
        k = 1 + t // pieces
        p = t % pieces

        @pl.when(b - k >= 0)
        def _():
            left(b - k, p, b + 1, up_sent)

        @pl.when(b + k < n)
        def _():
            left(b + k, p, b - 1, down_sent)

        return 0

    lax.fori_loop(0, count, sent_step, 0)


def local_distances(orbitals, offsets):
    n = lax.axis_size("blk")
    pieces = 2
    rows = orbitals.shape[1] // LANES
    quarter = rows // n
    chips = n // 2
    plane = NG * NG // LANES
    fills = pl.cdiv(plane, (n - 1) * pieces) * (n - 1) * pieces
    tables = cas_tables(NG)
    f32 = jnp.float32
    vmem = pl.BlockSpec(memory_space=pltpu.VMEM)
    dma = pltpu.SemaphoreType.DMA
    exchanged, margin = pl.pallas_call(
        functools.partial(exchange_kernel, n, pieces),
        out_shape=(
            jax.ShapeDtypeStruct((quarter, LANES), f32),
            jax.ShapeDtypeStruct((1, n), f32),
        ),
        in_specs=[pl.BlockSpec(memory_space=pltpu.SMEM)] + [vmem] * 5,
        out_specs=(vmem, vmem),
        scratch_shapes=[
            pltpu.VMEM((n, quarter, LANES), f32),
            pltpu.VMEM((rows, LANES), f32),
            pltpu.VMEM((rows, LANES), f32),
            pltpu.VMEM((fills * NG, LANES), f32),
            pltpu.VMEM((chips, quarter, LANES), f32),
            pltpu.VMEM((chips, quarter, LANES), f32),
            pltpu.VMEM((chips, quarter, LANES), f32),
            pltpu.VMEM((chips, quarter, LANES), f32),
            pltpu.VMEM((8, LANES), f32),
            pltpu.VMEM((n * n, 8, LANES), f32),
            dma((n, pieces)),
            dma((n, pieces)),
            dma((n, pieces)),
            dma((n, pieces)),
            dma((n, pieces)),
            dma((1 + pieces,)),
            dma((chips, pieces)),
            dma((chips, pieces)),
            dma((chips, pieces)),
            dma((chips, pieces)),
            dma((n * n,)),
            dma((n * n,)),
        ],
        compiler_params=pltpu.CompilerParams(
            collective_id=0, has_side_effects=True, vmem_limit_bytes=16 << 20
        ),
    )(offsets, orbitals.reshape(rows, LANES), *tables)
    return exchanged.reshape(1, quarter * LANES), margin


def solution(mesh):
    placed = (P(("groups", "blk"), None), P("groups"))
    one_each = mesh.shape["blk"] == mesh.shape["rep"] and mesh.shape["rep"] % 2 == 0
    local = local_distances if one_each else local_steps
    return jax.shard_map(
        local,
        mesh=mesh,
        in_specs=placed,
        out_specs=(P(("groups", "blk"), "rep"), P(("groups", "blk"), None)),
        check_vma=False,
    )
```
